32 devices in a mesh: section: 4 (over z), dp: 8 (over y, x, core).
Axes of the slice: x: 2, y: 2, z: 4, core: 2. Of those that a mesh axis runs over, the one named last changes fastest.
Arguments:
- acts: bfloat16 [4, 3072, 8192], P('section', 'dp'), may hold values from -6 to 6
- input_grads: bfloat16 [4, 3072, 5120], P('section', 'dp'), may hold values from -6 to 6
- head_grads: bfloat16 [3072, 5120], P('dp'), may hold values from -6 to 6
- weight_grad: bfloat16 [4, 5120, 8192], P('section', None, 'dp'), may hold values from -6 to 6
- sweeps: int32 [4, 52], P('section'), may hold values from 1 to 4
Outputs:
- update: bfloat16 [4, 5120, 8192], P('section', None, 'dp')
The draws below stay inside these ranges and needn't reach their ends.
Inputs may be any that keep to these rules, and one draw needn't show every extreme that they name: sweeps[s, k] is the number of Newton-Schulz iterations of block k of layer s; every value from 1 to 4 occurs.
All inputs are finite; a program needn't handle non-finite values. Where the reference program divides by a largest or mean magnitude, that divisor is 1e-20 or more.
Results may differ from the reference program's by a relative error of at most 0.0067.
Values may be sent and summed in bfloat16 or wider, within the bound.
No kernel may reach another device: no remote copies, remote signals or barrier semaphores. Data moves between devices by JAX's collectives and lax.ppermute only.
A program may use at most 128 MiB of HBM per device.

```python
import jax
import jax.numpy as jnp
from jax import lax

D = 5120
H = 8192
BLOCK = 256
NS_MAX = 4
SECTIONS = 4
TOKENS = 3072
NBLK = 52


def with_ends(values, rng, smallest, high):
    longest = values.shape.index(max(values.shape))
    spots = []
    for shift in (0, 1):
        where = [jax.random.randint(jax.random.fold_in(rng, axis), (), 0, length) for axis, length in enumerate(values.shape)]
        where[longest] = (where[longest] + shift) % values.shape[longest]
        spots.append(tuple(where))
    return values.at[spots[0]].set(smallest).at[spots[1]].set(high)


def steps_of(own_key, shape, cuts, low, top_value):
    level = 1.0
    for position, parts in cuts:
        steps = jax.random.uniform(jax.random.fold_in(jax.random.fold_in(own_key, 6), position), (parts,), jnp.float32, low / len(cuts), top_value / len(cuts))
        level = level * jnp.repeat(jnp.exp(steps), shape[position] // parts).reshape((-1,) + (1,) * (len(shape) - 1 - position))
    return level


def centred(rng, shape, deviation, bound, split=(), kind=jnp.bfloat16):
    level = steps_of(rng, shape, split, -0.22, 0.18) if split else 1.0
    drawn = jax.random.normal(rng, shape, jnp.float32) * deviation * level
    return jnp.minimum(jnp.maximum(drawn, -bound), bound).astype(kind)


def setup_inputs(seed: int = 0) -> dict:
    streams_of = jax.random.split(jax.random.key(seed), 6)
    return {
        "acts": centred(streams_of[0], (SECTIONS, TOKENS, H), 1.0, 6.0, ((0, 4), (1, 8))),
        "input_grads": centred(streams_of[1], (SECTIONS, TOKENS, D), 1.0, 6.0, ((0, 4), (1, 8))),
        "head_grads": centred(streams_of[2], (TOKENS, D), 1.0, 6.0, ((0, 8),)),
        "weight_grad": centred(streams_of[3], (SECTIONS, D, H), 1.0, 6.0, ((0, 4), (2, 8))),
        "sweeps": with_ends(jax.random.randint(streams_of[4], (SECTIONS, NBLK), 1, NS_MAX + 1), jax.random.fold_in(streams_of[4], 1), 1, NS_MAX).astype(jnp.int32),
    }


damping = 0.05


def newton_blocks(matrices, counts):
    size = matrices.shape[-1]
    eye = jnp.eye(size, dtype=jnp.float32)
    scale = 1.0 / jnp.max(jnp.sum(jnp.abs(matrices), axis=2), axis=1)
    approx = scale[:, None, None] * eye[None]
    for turn in range(NS_MAX):
        inner = 2.0 * eye[None] - jnp.einsum("kab,kbc->kac", matrices, approx, precision=lax.Precision.HIGHEST)
        fresh = jnp.einsum("kab,kbc->kac", approx, inner, precision=lax.Precision.HIGHEST)
        approx = jnp.where((turn < counts)[:, None, None], fresh, approx)
    return approx


def reference(acts, input_grads, head_grads, weight_grad, sweeps):
    eye = jnp.eye(BLOCK, dtype=jnp.float32)
    hidden_blocks = H // BLOCK
    model_blocks = D // BLOCK
    results = []
    for layer in range(SECTIONS):
        inputs = acts[layer].astype(jnp.float32).reshape(TOKENS, hidden_blocks, BLOCK)
        if layer + 1 < SECTIONS:
            grads = input_grads[layer + 1]
        else:
            grads = head_grads
        grads = grads.astype(jnp.float32).reshape(TOKENS, model_blocks, BLOCK)
        side_a = jnp.einsum("tkb,tkc->kbc", inputs, inputs, precision=lax.Precision.HIGHEST)
        side_g = jnp.einsum("tkb,tkc->kbc", grads, grads, precision=lax.Precision.HIGHEST)
        factors = jnp.concatenate([side_a, side_g], axis=0) / TOKENS + damping * eye[None]
        inverse = newton_blocks(factors, sweeps[layer]).astype(jnp.bfloat16)
        inverse_a = inverse[:hidden_blocks].astype(jnp.float32)
        inverse_g = inverse[hidden_blocks:].astype(jnp.float32)
        weights = weight_grad[layer].astype(jnp.float32).reshape(D, hidden_blocks, BLOCK)
        half = jnp.einsum("dkb,kbc->dkc", weights, inverse_a, precision=lax.Precision.HIGHEST).astype(jnp.bfloat16)
        half = half.reshape(model_blocks, BLOCK, H).astype(jnp.float32)
        update = jnp.einsum("kab,kbc->kac", inverse_g, half, precision=lax.Precision.HIGHEST)
        results.append(update.reshape(D, H).astype(jnp.bfloat16))
    return jnp.stack(results)
```

```python
import functools

import jax
import jax.numpy as jnp
from jax import lax
from jax.experimental import pallas as pl
from jax.experimental.pallas import tpu as pltpu
from jax.sharding import PartitionSpec as P

BLOCK = 256
HALF = BLOCK // 2
PAD = 16
NS_MAX = 4

damping = 0.05


def masks():
    row = lax.broadcasted_iota(jnp.int32, (HALF, HALF), 0)
    col = lax.broadcasted_iota(jnp.int32, (HALF, HALF), 1)
    return row, col


def pack_block(full, row, col):
    upper = full[:HALF, HALF:]
    second = full[HALF:, HALF:]
    mixed = jnp.where(row >= col, full[:HALF, :HALF], second)
    line = jnp.sum(jnp.where(row == col, second, 0.0), axis=0, keepdims=True)
    return upper, mixed, line


def unpack_block(upper, mixed, line, row, col):
    turned = mixed.T
    first = jnp.where(row >= col, mixed, turned)
    second = jnp.where(row < col, mixed, jnp.where(row > col, turned, line))
    top = jnp.concatenate([first, upper], axis=1)
    bottom = jnp.concatenate([upper.T, second], axis=1)
    return jnp.concatenate([top, bottom], axis=0)


def store_unit(out, index, blocks, row, col):
    count = len(blocks)
    lines = jnp.zeros((PAD, HALF), jnp.float32)
    place = lax.broadcasted_iota(jnp.int32, (PAD, HALF), 0)
    for j, full in enumerate(blocks):
        upper, mixed, line = pack_block(full, row, col)
        out[index + (pl.ds(j * BLOCK, HALF),)] = upper.astype(out.dtype)
        out[index + (pl.ds(j * BLOCK + HALF, HALF),)] = mixed.astype(out.dtype)
        lines = jnp.where(place == j, line, lines)
    out[index + (pl.ds(count * BLOCK, PAD),)] = lines.astype(out.dtype)


def gram(x):
    return lax.dot_general(x, x, (((0,), (0,)), ((), ())), preferred_element_type=jnp.float32)


def factor_kernel(slots, choices, place_ref, *refs):
    out = refs[-1]
    row, col = masks()

    def run(group):
        store_unit(out, (0,), [gram(ref[...]) for ref in group], row, col)

    if choices == 1:
        run(refs[:slots])
    else:
        pl.when(place_ref[1] == 0)(lambda: run(refs[:slots]))
        pl.when(place_ref[1] != 0)(lambda: run(refs[slots : 2 * slots]))


def partial_factors(place, sources, slots, block_of, parity, dp_count):
    unit = slots * BLOCK + PAD
    tokens = sources[0].shape[-2]
    steps = dp_count // 2

    def spec(which, slot):
        lead = (None,) * (sources[which].ndim - 2)

        def index(g, place_ref):
            owner = place_ref[0] ^ (2 * g + parity)
            block = block_of(owner, slot)
            if len(sources) > 1:
                block = jnp.where(place_ref[1] == which, block, 0)
            return (0,) * len(lead) + (0, block)

        return pl.BlockSpec(lead + (tokens, BLOCK), index)

    specs = [spec(which, slot) for which in range(len(sources)) for slot in range(slots)]
    operands = [source for source in sources for _ in range(slots)]
    return pl.pallas_call(
        functools.partial(factor_kernel, slots, len(sources)),
        out_shape=jax.ShapeDtypeStruct((steps, unit, HALF), jnp.bfloat16),
        grid_spec=pltpu.PrefetchScalarGridSpec(
            num_scalar_prefetch=1,
            grid=(steps,),
            in_specs=specs,
            out_specs=pl.BlockSpec((1, unit, HALF), lambda g, place_ref: (g, 0, 0)),
        ),
        cost_estimate=pl.CostEstimate(
            flops=2 * steps * slots * tokens * BLOCK * BLOCK,
            bytes_accessed=steps * slots * (tokens + HALF) * BLOCK * 2,
            transcendentals=0,
        ),
    )(place, *operands)


def split(a):
    high = a.astype(jnp.bfloat16)
    return high, (a - high.astype(jnp.float32)).astype(jnp.bfloat16)


def product(a, b):
    def dot(x, y):
        return jnp.dot(x, y, preferred_element_type=jnp.float32)

    return dot(a[0], b[0]) + (dot(a[0], b[1]) + dot(a[1], b[0]))


def newton(matrices, counts):
    row = lax.broadcasted_iota(jnp.int32, (BLOCK, BLOCK), 0)
    col = lax.broadcasted_iota(jnp.int32, (BLOCK, BLOCK), 1)
    eye = (row == col).astype(jnp.float32)
    rest, found = [], []
    for matrix in matrices:
        scale = 1.0 / jnp.max(jnp.sum(jnp.abs(matrix), axis=0, keepdims=True), axis=1, keepdims=True)
        left = eye - scale * matrix
        rest.append(left)
        found.append(scale * (eye + left))
    for turn in range(1, NS_MAX):
        parts = [split(left) for left in rest]
        rest = [product(part, part) for part in parts]
        squares = [split(left) for left in rest]
        step = [product(split(x), square) for x, square in zip(found, squares)]
        found = [jnp.where(turn < count, x + more, x) for x, more, count in zip(found, step, counts)]
    return found


def summed_factors(refs, slots, token_total, row, col):
    parts = []
    for ref in refs:
        parts.append(ref[0] if len(ref.shape) == 3 else ref[...])
    total = sum(part.astype(jnp.float32) for part in parts) * (1.0 / token_total)
    wide_row = lax.broadcasted_iota(jnp.int32, (BLOCK, BLOCK), 0)
    wide_col = lax.broadcasted_iota(jnp.int32, (BLOCK, BLOCK), 1)
    shift = jnp.where(wide_row == wide_col, damping, 0.0)
    blocks = []
    for j in range(slots):
        upper = total[j * BLOCK : j * BLOCK + HALF]
        mixed = total[j * BLOCK + HALF : (j + 1) * BLOCK]
        line = total[slots * BLOCK + j : slots * BLOCK + j + 1]
        blocks.append(unpack_block(upper, mixed, line, row, col) + shift)
    return blocks


def invert_kernel(slots, token_total, count_ref, *refs):
    out = refs[-1]
    row, col = masks()
    blocks = summed_factors(refs[:-1], slots, token_total, row, col)
    found = newton(blocks, [count_ref[j] for j in range(slots)])
    store_unit(out, (), found, row, col)


def unit_specs(own, first, others):
    unit = own.shape[1]
    front = pl.BlockSpec((1, unit, HALF), lambda g, *_: (0, 0, 0))
    whole = pl.BlockSpec((unit, HALF), lambda g, *_: (0, 0))
    return [front, front] + [whole] * len(others)


def invert_units(counts, own, first, others, slots, token_total):
    unit = own.shape[1]
    return pl.pallas_call(
        functools.partial(invert_kernel, slots, token_total),
        out_shape=jax.ShapeDtypeStruct((unit, HALF), jnp.bfloat16),
        grid_spec=pltpu.PrefetchScalarGridSpec(
            num_scalar_prefetch=1,
            grid=(1,),
            in_specs=unit_specs(own, first, others),
            out_specs=pl.BlockSpec((unit, HALF), lambda g, *_: (0, 0)),
        ),
        cost_estimate=pl.CostEstimate(
            flops=36 * slots * BLOCK**3, bytes_accessed=12 * slots * BLOCK * BLOCK, transcendentals=0
        ),
    )(counts, own, first, *others)


def half_kernel(slots, token_total, count_ref, *refs):
    weights, out, inverse = refs[-3:]
    rows = weights.shape[0]

    @pl.when(pl.program_id(0) == 0)
    def _():
        row, col = masks()
        blocks = summed_factors(refs[:-3], slots, token_total, row, col)
        found = newton(blocks, [count_ref[j] for j in range(slots)])
        for j in range(slots):
            inverse[j] = found[j].astype(jnp.bfloat16)

    place = pl.ds(pl.multiple_of(pl.program_id(0) * rows, rows), rows)
    for j in range(slots):
        columns = slice(j * BLOCK, (j + 1) * BLOCK)
        value = jnp.dot(weights[:, columns], inverse[j], preferred_element_type=jnp.float32)
        out[place, columns] = value.astype(jnp.bfloat16)


def half_update(counts, own, first, others, slots, token_total, weight_grad):
    _, depth, columns = weight_grad.shape
    rows = 2 * BLOCK
    specs = unit_specs(own, first, others)
    specs.append(pl.BlockSpec((None, rows, columns), lambda g, *_: (0, g, 0)))
    return pl.pallas_call(
        functools.partial(half_kernel, slots, token_total),
        out_shape=jax.ShapeDtypeStruct((depth, columns), jnp.bfloat16),
        grid_spec=pltpu.PrefetchScalarGridSpec(
            num_scalar_prefetch=1,
            grid=(depth // rows,),
            in_specs=specs,
            out_specs=pl.BlockSpec(memory_space=pltpu.VMEM),
            scratch_shapes=[pltpu.VMEM((slots, BLOCK, BLOCK), jnp.bfloat16)],
        ),
        cost_estimate=pl.CostEstimate(
            flops=36 * slots * BLOCK**3 + 2 * depth * columns * BLOCK,
            bytes_accessed=2 * depth * columns,
            transcendentals=0,
        ),
    )(counts, own, first, *others, weight_grad)


def update_kernel(slots, dp_count, place_ref, *refs):
    half, out, inverse = refs[-3:]
    groups = refs[:-3]
    k = pl.program_id(0)

    @pl.when(k == 0)
    def _():
        row, col = masks()
        units = []
        for ref in groups:
            units += [ref[i] for i in range(ref.shape[0])] if len(ref.shape) == 3 else [ref[...]]
        for r, unit in zip(list(range(0, dp_count, 2)) + list(range(1, dp_count, 2)), units):
            owner = place_ref[0] ^ r
            unit = unit.astype(jnp.float32)
            for j in range(slots):
                upper = unit[j * BLOCK : j * BLOCK + HALF]
                mixed = unit[j * BLOCK + HALF : (j + 1) * BLOCK]
                line = unit[slots * BLOCK + j : slots * BLOCK + j + 1]
                full = unpack_block(upper, mixed, line, row, col)
                inverse[owner + dp_count * j] = full.astype(jnp.bfloat16)

    place = pl.ds(pl.multiple_of(k * BLOCK, BLOCK), BLOCK)
    value = jnp.dot(inverse[k], half[place, :], preferred_element_type=jnp.float32)
    out[...] = value.astype(jnp.bfloat16)


def final_update(place, units, half, slots, dp_count):
    depth, columns = half.shape
    blocks = depth // BLOCK
    return pl.pallas_call(
        functools.partial(update_kernel, slots, dp_count),
        out_shape=jax.ShapeDtypeStruct((1, depth, columns), jnp.bfloat16),
        grid_spec=pltpu.PrefetchScalarGridSpec(
            num_scalar_prefetch=1,
            grid=(blocks,),
            in_specs=[pl.BlockSpec(memory_space=pltpu.VMEM)] * (len(units) + 1),
            out_specs=pl.BlockSpec((None, BLOCK, columns), lambda g, *_: (0, g, 0)),
            scratch_shapes=[pltpu.VMEM((dp_count * slots, BLOCK, BLOCK), jnp.bfloat16)],
        ),
        cost_estimate=pl.CostEstimate(
            flops=2 * depth * columns * BLOCK, bytes_accessed=2 * depth * columns, transcendentals=0
        ),
    )(place, *units, half)


def swap(value, distance):
    count = lax.axis_size("dp")
    return lax.ppermute(value, "dp", [(i, i ^ distance) for i in range(count)])


def scattered(send, keep, dp_count):
    first = swap(send, 1)
    others = []
    for r in range(2, dp_count, 2):
        value = keep[r // 2].astype(jnp.float32) + first[r // 2].astype(jnp.float32)
        others.append(swap(value.astype(jnp.bfloat16), r))
    return first, others


def on_device(acts, input_grads, head_grads, weight_grad, sweeps):
    dp_count = lax.axis_size("dp")
    me = lax.axis_index("dp")
    section_count = lax.axis_size("section")
    section_index = lax.axis_index("section")
    tokens = acts.shape[1] * dp_count
    hidden_blocks = acts.shape[2] // BLOCK
    model_blocks = input_grads.shape[2] // BLOCK
    slots_a = hidden_blocks // dp_count
    slots_g = -(-model_blocks // dp_count)

    is_first = (section_index == 0).astype(jnp.int32)
    place = jnp.stack([me, is_first]).astype(jnp.int32)
    back = [((s + 1) % section_count, s) for s in range(section_count)]
    ahead = [(s, (s + 1) % section_count) for s in range(section_count)]
    their_sweeps = lax.ppermute(sweeps, "section", ahead)[0]

    def block_g(owner, slot):
        return jnp.minimum(owner + dp_count * slot, model_blocks - 1)

    def block_a(owner, slot):
        return owner * slots_a + slot

    grads = [input_grads, head_grads]
    send_g = partial_factors(place, grads, slots_g, block_g, 1, dp_count)
    keep_g = partial_factors(place, grads, slots_g, block_g, 0, dp_count)
    first_g, others_g = scattered(send_g, keep_g, dp_count)
    send_a = partial_factors(place, [acts], slots_a, block_a, 1, dp_count)
    keep_a = partial_factors(place, [acts], slots_a, block_a, 0, dp_count)
    first_a, others_a = scattered(send_a, keep_a, dp_count)

    slot_ids = jnp.arange(slots_g, dtype=jnp.int32)
    count_g = jnp.take(their_sweeps, hidden_blocks + block_g(me, slot_ids))
    count_a = lax.dynamic_slice_in_dim(sweeps[0], me * slots_a, slots_a)
    unit = invert_units(count_g, keep_g, first_g, others_g, slots_g, tokens)
    unit = lax.ppermute(unit, "section", back)
    even = [unit] + [swap(unit, r) for r in range(2, dp_count, 2)]
    odd = [swap(value, 1) for value in even]

    half = half_update(count_a, keep_a, first_a, others_a, slots_a, tokens, weight_grad)
    return final_update(place, even + odd, half, slots_g, dp_count)


def solution(mesh):
    return jax.shard_map(
        on_device,
        mesh=mesh,
        in_specs=(
            P("section", "dp", None),
            P("section", "dp", None),
            P("dp", None),
            P("section", None, "dp"),
            P("section", None),
        ),
        out_specs=P("section", None, "dp"),
        check_vma=False,
    )
```

```python
import functools

import jax
import jax.numpy as jnp
from jax import lax
from jax.experimental import pallas as pl
from jax.experimental.pallas import tpu as pltpu
from jax.sharding import PartitionSpec as P


BLOCK = 256
HALF = BLOCK // 2
PAD = 16
NS_MAX = 4

damping = 0.05


def masks():
    row = lax.broadcasted_iota(jnp.int32, (HALF, HALF), 0)
    col = lax.broadcasted_iota(jnp.int32, (HALF, HALF), 1)
    return row, col


def pack_block(full, row, col):
    upper = full[:HALF, HALF:]
    second = full[HALF:, HALF:]
    mixed = jnp.where(row >= col, full[:HALF, :HALF], second)
    line = jnp.sum(jnp.where(row == col, second, 0.0), axis=0, keepdims=True)
    return upper, mixed, line


def unpack_block(upper, mixed, line, row, col):
    turned = mixed.T
    first = jnp.where(row >= col, mixed, turned)
    second = jnp.where(row < col, mixed, jnp.where(row > col, turned, line))
    top = jnp.concatenate([first, upper], axis=1)
    bottom = jnp.concatenate([upper.T, second], axis=1)
    return jnp.concatenate([top, bottom], axis=0)


def store_unit(out, index, blocks, row, col):
    count = len(blocks)
    lines = jnp.zeros((PAD, HALF), jnp.float32)
    place = lax.broadcasted_iota(jnp.int32, (PAD, HALF), 0)
    for j, full in enumerate(blocks):
        upper, mixed, line = pack_block(full, row, col)
        out[index + (pl.ds(j * BLOCK, HALF),)] = upper.astype(out.dtype)
        out[index + (pl.ds(j * BLOCK + HALF, HALF),)] = mixed.astype(out.dtype)
        lines = jnp.where(place == j, line, lines)
    out[index + (pl.ds(count * BLOCK, PAD),)] = lines.astype(out.dtype)


def gram(x):
    return lax.dot_general(x, x, (((0,), (0,)), ((), ())), preferred_element_type=jnp.float32)


def shares(blocks, dp_count):
    share, rest = blocks // dp_count, blocks % dp_count
    return share, -(-rest // (dp_count // 2))


def owned_block(owner, slot, blocks, dp_count):
    share, _ = shares(blocks, dp_count)
    if slot < share:
        return owner * share + slot
    chips = dp_count // 2
    return jnp.minimum(share * dp_count + owner // 2 + chips * (slot - share), blocks - 1)


def factor_kernel(blocks, dp_count, parities, choices, keep, *refs):
    slots = sum(shares(blocks, dp_count))
    me = lax.axis_index("dp")
    sources = refs[: max(choices, 1)]
    if choices:
        sems, columns = refs[-1], refs[-2]
        outs = refs[-2 - len(parities) : -2]
        chunks = sems.shape[0]
        rows = columns.shape[0] // chunks

        def fetch(source, i):
            place = pl.ds(i * rows, rows)
            view = source.at[0, place] if len(source.shape) == 3 else source.at[place]
            return pltpu.make_async_copy(view, columns.at[place], sems.at[i])

        def fetch_all(source):
            for i in range(chunks):
                fetch(source, i).start()

        if choices == 1:
            fetch_all(sources[0])
        else:
            first = lax.axis_index("section") == 0
            pl.when(first)(lambda: fetch_all(sources[1]))
            pl.when(jnp.logical_not(first))(lambda: fetch_all(sources[0]))
        for i in range(chunks):
            fetch(sources[0], i).wait()
    else:
        columns, outs = refs[0], refs[-len(parities) :]
    row, col = masks()
    for parity, out in zip(parities, outs):
        for step in range(dp_count // 2):
            grams = []
            for slot in range(slots):
                block = owned_block(me ^ (2 * step + parity), slot, blocks, dp_count)
                place = pl.ds(pl.multiple_of(block * BLOCK, BLOCK), BLOCK)
                grams.append(gram(columns[:, place]))
            store_unit(out, (step,), grams, row, col)


def partial_factors(sources, dp_count, parities, keep=False, loaded=False, after=()):
    tokens, width = sources[0].shape[-2:]
    blocks = width // BLOCK
    unit = sum(shares(blocks, dp_count)) * BLOCK + PAD
    outs = [pltpu.VMEM((dp_count // 2, unit, HALF), jnp.bfloat16)] * len(parities)
    columns = pltpu.VMEM((tokens, width), jnp.bfloat16)
    vmem = pl.BlockSpec(memory_space=pltpu.VMEM)
    scratch = [] if loaded else [pltpu.SemaphoreType.DMA((4,))]
    if keep:
        outs.append(columns)
    elif not loaded:
        scratch.insert(0, columns)
    space = pltpu.VMEM if loaded else pltpu.HBM
    specs = [pl.BlockSpec(memory_space=space)] * len(sources)
    return pl.pallas_call(
        functools.partial(
            factor_kernel, blocks, dp_count, parities, 0 if loaded else len(sources), keep
        ),
        out_shape=tuple(outs),
        in_specs=specs + [pl.BlockSpec(memory_space=pl.ANY)] * len(after),
        out_specs=tuple([vmem] * len(outs)),
        scratch_shapes=scratch,
        compiler_params=pltpu.CompilerParams(vmem_limit_bytes=20 << 20),
        cost_estimate=pl.CostEstimate(
            flops=len(parities) * tokens * width * BLOCK,
            bytes_accessed=tokens * width * 3,
            transcendentals=0,
        ),
    )(*[pltpu.with_memory_space_constraint(source, space) for source in sources], *after)


def split(a):
    high = a.astype(jnp.bfloat16)
    return high, (a - high.astype(jnp.float32)).astype(jnp.bfloat16)


def product(a, b):
    def dot(x, y):
        return jnp.dot(x, y, preferred_element_type=jnp.float32)

    return dot(a[0], b[0]) + (dot(a[0], b[1]) + dot(a[1], b[0]))


def newton(matrices, counts):
    row = lax.broadcasted_iota(jnp.int32, (BLOCK, BLOCK), 0)
    col = lax.broadcasted_iota(jnp.int32, (BLOCK, BLOCK), 1)
    eye = (row == col).astype(jnp.float32)
    rest, found = [], []
    for matrix in matrices:
        scale = 1.0 / jnp.max(jnp.sum(jnp.abs(matrix), axis=0, keepdims=True), axis=1, keepdims=True)
        left = eye - scale * matrix
        rest.append(left)
        found.append(scale * (eye + left))
    for turn in range(1, NS_MAX):
        parts = [split(left) for left in rest]
        rest = [product(part, part) for part in parts]
        squares = [split(left) for left in rest]
        step = [product(split(x), square) for x, square in zip(found, squares)]
        found = [jnp.where(turn < count, x + more, x) for x, more, count in zip(found, step, counts)]
    return found


def summed_factors(refs, slots, token_total, row, col):
    parts = []
    for ref in refs:
        parts.append(ref[0] if len(ref.shape) == 3 else ref[...])
    total = sum(part.astype(jnp.float32) for part in parts) * (1.0 / token_total)
    wide_row = lax.broadcasted_iota(jnp.int32, (BLOCK, BLOCK), 0)
    wide_col = lax.broadcasted_iota(jnp.int32, (BLOCK, BLOCK), 1)
    shift = jnp.where(wide_row == wide_col, damping, 0.0)
    blocks = []
    for j in range(slots):
        upper = total[j * BLOCK : j * BLOCK + HALF]
        mixed = total[j * BLOCK + HALF : (j + 1) * BLOCK]
        line = total[slots * BLOCK + j : slots * BLOCK + j + 1]
        blocks.append(unpack_block(upper, mixed, line, row, col) + shift)
    return blocks


def gather_rows(blocks, dp_count):
    share, extra = shares(blocks, dp_count)
    return share * BLOCK + extra * HALF + PAD


def invert_kernel(hidden_blocks, blocks, dp_count, token_total, sweeps, *refs):
    out = refs[-1]
    row, col = masks()
    share, extra = shares(blocks, dp_count)
    slots = share + extra
    me = lax.axis_index("dp")
    factors = summed_factors(refs[:-1], slots, token_total, row, col)
    counts = [
        sweeps[0, hidden_blocks + owned_block(me, j, blocks, dp_count)] for j in range(slots)
    ]
    lines = jnp.zeros((PAD, HALF), jnp.float32)
    place = lax.broadcasted_iota(jnp.int32, (PAD, HALF), 0)
    even = me % 2 == 0
    for j, full in enumerate(newton(factors, counts)):
        upper, mixed, line = pack_block(full, row, col)
        lines = jnp.where(place == j, line, lines)
        if j < share:
            out[pl.ds(j * BLOCK, HALF)] = upper.astype(out.dtype)
            out[pl.ds(j * BLOCK + HALF, HALF)] = mixed.astype(out.dtype)
        else:
            own = jnp.where(even, upper, mixed)
            out[pl.ds(share * BLOCK + (j - share) * HALF, HALF)] = own.astype(out.dtype)
    out[pl.ds(share * BLOCK + extra * HALF, PAD)] = lines.astype(out.dtype)


def unit_specs(own, others):
    unit = own.shape[1]
    front = pl.BlockSpec((1, unit, HALF), lambda g, *_: (0, 0, 0))
    whole = pl.BlockSpec((unit, HALF), lambda g, *_: (0, 0))
    return [front, front] + [whole] * len(others)


def invert_units(sweeps, own, first, others, hidden_blocks, blocks, dp_count, token_total):
    unit = gather_rows(blocks, dp_count)
    slots = sum(shares(blocks, dp_count))
    return pl.pallas_call(
        functools.partial(invert_kernel, hidden_blocks, blocks, dp_count, token_total),
        out_shape=jax.ShapeDtypeStruct((unit, HALF), jnp.bfloat16),
        grid_spec=pltpu.PrefetchScalarGridSpec(
            num_scalar_prefetch=1,
            grid=(1,),
            in_specs=unit_specs(own, others),
            out_specs=pl.BlockSpec((unit, HALF), lambda g, *_: (0, 0)),
        ),
        compiler_params=pltpu.CompilerParams(vmem_limit_bytes=16 << 20),
        cost_estimate=pl.CostEstimate(
            flops=36 * slots * BLOCK**3, bytes_accessed=12 * slots * BLOCK * BLOCK, transcendentals=0
        ),
    )(sweeps, own, first, *others)


def half_kernel(slots, token_total, sweeps, *refs):
    weights, out = refs[-2:]
    row, col = masks()
    me = lax.axis_index("dp")
    factors = summed_factors(refs[:-2], slots, token_total, row, col)
    found = newton(factors, [sweeps[0, me * slots + j] for j in range(slots)])
    for j in range(slots):
        columns = slice(j * BLOCK, (j + 1) * BLOCK)
        value = jnp.dot(
            weights[0, :, columns],
            found[j].astype(jnp.bfloat16),
            preferred_element_type=jnp.float32,
        )
        out[:, columns] = value.astype(jnp.bfloat16)


def half_update(sweeps, own, first, others, token_total, weight_grad):
    _, depth, columns = weight_grad.shape
    slots = columns // BLOCK
    specs = unit_specs(own, others) + [pl.BlockSpec(memory_space=pltpu.VMEM)]
    return pl.pallas_call(
        functools.partial(half_kernel, slots, token_total),
        out_shape=pltpu.VMEM((depth, columns), jnp.bfloat16),
        grid_spec=pltpu.PrefetchScalarGridSpec(
            num_scalar_prefetch=1,
            grid=(1,),
            in_specs=specs,
            out_specs=pl.BlockSpec(memory_space=pltpu.VMEM),
        ),
        compiler_params=pltpu.CompilerParams(vmem_limit_bytes=30 << 20),
        cost_estimate=pl.CostEstimate(
            flops=36 * slots * BLOCK**3 + 2 * depth * columns * BLOCK,
            bytes_accessed=2 * depth * columns,
            transcendentals=0,
        ),
    )(sweeps, own, first, *others, pltpu.with_memory_space_constraint(weight_grad, pltpu.VMEM))


def update_kernel(blocks, dp_count, *refs):
    half, out, staged, sems = refs[-4:]
    units = refs[:-4]
    share, extra = shares(blocks, dp_count)
    me = lax.axis_index("dp")
    row, col = masks()
    even = me % 2 == 0

    def copy(step, block):
        place = pl.ds(pl.multiple_of(block * BLOCK, BLOCK), BLOCK)
        return pltpu.make_async_copy(staged.at[step], out.at[0, place], sems.at[step])

    def tile(unit, start, rows=HALF):
        return unit[start : start + rows, :].astype(jnp.float32)

    def one(step, r, slot):
        near, far = units[r // 2], units[(dp_count + r) // 2]
        owner = me ^ r
        if slot >= 2 * share:
            slot -= share
            start = share * BLOCK + (slot - share) * HALF
            own, other = tile(near, start), tile(far, start)
            upper, mixed = jnp.where(even, own, other), jnp.where(even, other, own)
        else:
            if slot >= share:
                near, owner, slot = far, owner ^ 1, slot - share
            upper, mixed = tile(near, slot * BLOCK), tile(near, slot * BLOCK + HALF)
        block = owned_block(owner, slot, blocks, dp_count)
        line = tile(near, share * BLOCK + extra * HALF, PAD)[slot : slot + 1]
        full = unpack_block(upper, mixed, line, row, col).astype(jnp.bfloat16)
        place = pl.ds(pl.multiple_of(block * BLOCK, BLOCK), BLOCK)
        value = jnp.dot(full, half[place, :], preferred_element_type=jnp.float32)
        staged[step] = value.astype(jnp.bfloat16)
        copy(step, block).start()

    def guarded(r, slot, run):
        chips, rest = dp_count // 2, blocks % dp_count
        if slot < 2 * share or rest == chips * extra:
            run()
        else:
            pl.when((me ^ r) // 2 + chips * (slot - 2 * share) < rest)(run)

    steps = [(r, slot) for r in range(0, dp_count, 2) for slot in range(2 * share + extra)]
    for step, (r, slot) in enumerate(steps):
        guarded(r, slot, functools.partial(one, step, r, slot))
    for step, (r, slot) in enumerate(steps):
        guarded(r, slot, lambda: copy(step, 0).wait())


def final_update(units, half, dp_count):
    depth, columns = half.shape
    blocks = depth // BLOCK
    share, extra = shares(blocks, dp_count)
    steps = dp_count // 2 * (2 * share + extra)
    return pl.pallas_call(
        functools.partial(update_kernel, blocks, dp_count),
        out_shape=jax.ShapeDtypeStruct((1, depth, columns), jnp.bfloat16),
        in_specs=[pl.BlockSpec(memory_space=pltpu.VMEM)] * (len(units) + 1),
        out_specs=pl.BlockSpec(memory_space=pl.ANY),
        scratch_shapes=[
            pltpu.VMEM((steps, BLOCK, columns), jnp.bfloat16),
            pltpu.SemaphoreType.DMA((steps,)),
        ],
        compiler_params=pltpu.CompilerParams(vmem_limit_bytes=30 << 20),
        cost_estimate=pl.CostEstimate(
            flops=2 * depth * columns * BLOCK, bytes_accessed=2 * depth * columns, transcendentals=0
        ),
    )(*units, pltpu.with_memory_space_constraint(half, pltpu.VMEM))


def swap(value, distance):
    count = lax.axis_size("dp")
    return lax.ppermute(value, "dp", [(i, i ^ distance) for i in range(count)])


def spread(keep, first, dp_count):
    others = []
    for r in range(2, dp_count, 2):
        value = keep[r // 2].astype(jnp.float32) + first[r // 2].astype(jnp.float32)
        others.append(swap(value.astype(jnp.bfloat16), r))
    return others


def whole(acts, input_grads, head_grads, weight_grad, sweeps):
    dp_count = lax.axis_size("dp")
    section_count = lax.axis_size("section")
    tokens = acts.shape[1] * dp_count
    hidden_blocks = acts.shape[2] // BLOCK
    model_blocks = input_grads.shape[2] // BLOCK
    back = [((s + 1) % section_count, s) for s in range(section_count)]
    ahead = [(s, (s + 1) % section_count) for s in range(section_count)]

    send_g, grads = partial_factors([input_grads, head_grads], dp_count, (1,), keep=True)
    first_g = swap(send_g, 1)
    (keep_g,) = partial_factors([grads], dp_count, (0,), loaded=True)
    their_sweeps = lax.ppermute(sweeps, "section", ahead)
    send_a, keep_a = partial_factors([acts], dp_count, (1, 0), after=(keep_g,))
    others_g = spread(keep_g, first_g, dp_count)
    first_a = swap(send_a, 1)
    unit = invert_units(
        their_sweeps, keep_g, first_g, others_g, hidden_blocks, model_blocks, dp_count, tokens
    )
    others_a = spread(keep_a, first_a, dp_count)
    unit = lax.ppermute(unit, "section", back)
    even = [unit] + [swap(unit, r) for r in range(2, dp_count, 2)]
    half = half_update(sweeps, keep_a, first_a, others_a, tokens, weight_grad)
    odd = [swap(value, 1) for value in even]
    return final_update(even + odd, half, dp_count)


def solution(mesh):
    return jax.shard_map(
        whole,
        mesh=mesh,
        in_specs=(
            P("section", "dp", None),
            P("section", "dp", None),
            P("dp", None),
            P("section", None, "dp"),
            P("section", None),
        ),
        out_specs=P("section", None, "dp"),
        check_vma=False,
    )
```

```python
import functools

import jax
import jax.numpy as jnp
from jax import lax
from jax.experimental import pallas as pl
from jax.experimental.pallas import tpu as pltpu
from jax.sharding import PartitionSpec as P


BLOCK = 256
HALF = BLOCK // 2
PAD = 16
NS_MAX = 4

damping = 0.05


def masks():
    row = lax.broadcasted_iota(jnp.int32, (HALF, HALF), 0)
    col = lax.broadcasted_iota(jnp.int32, (HALF, HALF), 1)
    return row, col


def pack_block(full, row, col):
    upper = full[:HALF, HALF:]
    second = full[HALF:, HALF:]
    mixed = jnp.where(row >= col, full[:HALF, :HALF], second)
    line = jnp.sum(jnp.where(row == col, second, 0.0), axis=0, keepdims=True)
    return upper, mixed, line


def unpack_block(upper, mixed, line, row, col):
    turned = mixed.T
    first = jnp.where(row >= col, mixed, turned)
    second = jnp.where(row < col, mixed, jnp.where(row > col, turned, line))
    top = jnp.concatenate([first, upper], axis=1)
    bottom = jnp.concatenate([upper.T, second], axis=1)
    return jnp.concatenate([top, bottom], axis=0)


def store_unit(out, index, blocks, row, col):
    count = len(blocks)
    lines = jnp.zeros((PAD, HALF), jnp.float32)
    place = lax.broadcasted_iota(jnp.int32, (PAD, HALF), 0)
    for j, full in enumerate(blocks):
        upper, mixed, line = pack_block(full, row, col)
        out[index + (pl.ds(j * BLOCK, HALF),)] = upper.astype(out.dtype)
        out[index + (pl.ds(j * BLOCK + HALF, HALF),)] = mixed.astype(out.dtype)
        lines = jnp.where(place == j, line, lines)
    out[index + (pl.ds(count * BLOCK, PAD),)] = lines.astype(out.dtype)


def gram(x):
    return lax.dot_general(x, x, (((0,), (0,)), ((), ())), preferred_element_type=jnp.float32)


def shares(blocks, dp_count):
    share, rest = blocks // dp_count, blocks % dp_count
    return share, -(-rest // (dp_count // 2))


def owned_block(owner, slot, blocks, dp_count):
    share, _ = shares(blocks, dp_count)
    if slot < share:
        return owner * share + slot
    chips = dp_count // 2
    return jnp.minimum(share * dp_count + owner // 2 + chips * (slot - share), blocks - 1)


def store_factors(columns, out, parity, blocks, dp_count, row, col):
    me = lax.axis_index("dp")
    for step in range(dp_count // 2):
        grams = []
        for slot in range(sum(shares(blocks, dp_count))):
            block = owned_block(me ^ (2 * step + parity), slot, blocks, dp_count)
            place = pl.ds(pl.multiple_of(block * BLOCK, BLOCK), BLOCK)
            grams.append(sum(gram(part[:, place]) for part in columns))
        store_unit(out, (step,), grams, row, col)


def send_kernel(blocks, dp_count, here, head, sent, grads, sems):
    chunks = sems.shape[0]
    rows = grads.shape[0] // chunks

    def fetch(source, i):
        place = pl.ds(i * rows, rows)
        view = source.at[0, place] if len(source.shape) == 3 else source.at[place]
        return pltpu.make_async_copy(view, grads.at[place], sems.at[i])

    def fetch_all(source):
        for i in range(chunks):
            fetch(source, i).start()

    first = lax.axis_index("section") == 0
    pl.when(first)(lambda: fetch_all(head))
    pl.when(jnp.logical_not(first))(lambda: fetch_all(here))
    for i in range(chunks):
        fetch(here, i).wait()
    store_factors([grads], sent, 1, blocks, dp_count, *masks())


def keep_kernel(blocks, dp_count, grads, acts, kept, early, sem):
    ahead = pltpu.make_async_copy(acts.at[0, pl.ds(0, early.shape[0])], early, sem)
    ahead.start()
    store_factors([grads], kept, 0, blocks, dp_count, *masks())
    ahead.wait()


def late_kernel(blocks, dp_count, early, acts, sent, late, sem):
    rows = late.shape[0]
    copy = pltpu.make_async_copy(acts.at[0, pl.ds(acts.shape[1] - rows, rows)], late, sem)
    copy.start()
    copy.wait()
    store_factors([early, late], sent, 1, blocks, dp_count, *masks())


def last_kernel(blocks, dp_count, early, late, kept):
    store_factors([early, late], kept, 0, blocks, dp_count, *masks())


def packed_shape(blocks, dp_count):
    unit = sum(shares(blocks, dp_count)) * BLOCK + PAD
    return pltpu.VMEM((dp_count // 2, unit, HALF), jnp.bfloat16)


def factor_call(kernel, operands, spaces, outs, scratch, rows, width, part):
    return pl.pallas_call(
        kernel,
        out_shape=outs,
        in_specs=[pl.BlockSpec(memory_space=space) for space in spaces],
        out_specs=tuple(pl.BlockSpec(memory_space=pltpu.VMEM) for _ in outs),
        scratch_shapes=scratch,
        compiler_params=pltpu.CompilerParams(vmem_limit_bytes=16 << 20),
        cost_estimate=pl.CostEstimate(
            flops=int(2 * part * rows * width * BLOCK), bytes_accessed=rows * width * 3, transcendentals=0
        ),
    )(
        *[
            pltpu.with_memory_space_constraint(operand, space)
            for operand, space in zip(operands, spaces)
        ]
    )


def model_factors(input_grads, head_grads, acts, dp_count):
    rows, width = head_grads.shape
    blocks = width // BLOCK
    early = rows // 3 // PAD * PAD
    hbm, vmem = pltpu.HBM, pltpu.VMEM
    packed = packed_shape(blocks, dp_count)
    sent, grads = factor_call(
        functools.partial(send_kernel, blocks, dp_count),
        [input_grads, head_grads],
        [hbm] * 2,
        (packed, pltpu.VMEM((rows, width), jnp.bfloat16)),
        [pltpu.SemaphoreType.DMA((4,))],
        rows,
        width,
        0.5,
    )
    kept, first = factor_call(
        functools.partial(keep_kernel, blocks, dp_count),
        [grads, acts],
        [vmem, hbm],
        (packed, pltpu.VMEM((early, acts.shape[2]), jnp.bfloat16)),
        [pltpu.SemaphoreType.DMA],
        rows,
        width,
        0.5,
    )
    return sent, kept, first


def hidden_factors(early, acts, dp_count):
    _, rows, width = acts.shape
    blocks = width // BLOCK
    packed = packed_shape(blocks, dp_count)
    vmem = pltpu.VMEM
    sent, late = factor_call(
        functools.partial(late_kernel, blocks, dp_count),
        [early, acts],
        [vmem, pltpu.HBM],
        (packed, pltpu.VMEM((rows - early.shape[0], width), jnp.bfloat16)),
        [pltpu.SemaphoreType.DMA],
        rows,
        width,
        0.5,
    )
    (kept,) = factor_call(
        functools.partial(last_kernel, blocks, dp_count),
        [early, late],
        [vmem] * 2,
        (packed,),
        [],
        rows,
        width,
        0.5,
    )
    return sent, kept


def product(a, b):
    return jnp.dot(
        a.astype(jnp.bfloat16), b.astype(jnp.bfloat16), preferred_element_type=jnp.float32
    )


def newton(matrices, counts):
    row = lax.broadcasted_iota(jnp.int32, (BLOCK, BLOCK), 0)
    col = lax.broadcasted_iota(jnp.int32, (BLOCK, BLOCK), 1)
    diagonal = row == col
    levels, rest, heights, found = [], [], [], []
    for matrix in matrices:
        size = jnp.sum(jnp.abs(matrix), axis=0, keepdims=True)
        scale = 1.0 / jnp.max(size, axis=1, keepdims=True)
        line = jnp.sum(jnp.where(diagonal, matrix, 0.0), axis=0, keepdims=True)
        shift = scale * jnp.sum(line, axis=1, keepdims=True) * (1.0 / BLOCK)
        left = jnp.where(diagonal, shift, 0.0) - scale * matrix
        levels.append(1.0 - shift)
        rest.append(left)
        heights.append(scale * (2.0 - shift))
        found.append(scale * left)
    for turn in range(1, NS_MAX):
        rest = [2.0 * a * left + product(left, left) for a, left in zip(levels, rest)]
        levels = [a * a for a in levels]
        step = [
            x * left + a * part + product(part, left)
            for a, left, x, part in zip(levels, rest, heights, found)
        ]
        more = [turn < count for count in counts]
        found = [jnp.where(go, part + add, part) for go, part, add in zip(more, found, step)]
        heights = [jnp.where(go, x + a * x, x) for go, x, a in zip(more, heights, levels)]
    return [part + jnp.where(diagonal, x, 0.0) for x, part in zip(heights, found)]


def summed_factors(refs, slots, token_total, row, col):
    terms = [ref[0] if len(ref.shape) == 3 else ref[...] for ref in refs]
    total = sum(term.astype(jnp.float32) for term in terms) * (1.0 / token_total)
    wide_row = lax.broadcasted_iota(jnp.int32, (BLOCK, BLOCK), 0)
    wide_col = lax.broadcasted_iota(jnp.int32, (BLOCK, BLOCK), 1)
    shift = jnp.where(wide_row == wide_col, damping, 0.0)
    blocks = []
    for j in range(slots):
        upper = total[j * BLOCK : j * BLOCK + HALF]
        mixed = total[j * BLOCK + HALF : (j + 1) * BLOCK]
        line = total[slots * BLOCK + j : slots * BLOCK + j + 1]
        blocks.append(unpack_block(upper, mixed, line, row, col) + shift)
    return blocks


def gather_rows(blocks, dp_count):
    share, extra = shares(blocks, dp_count)
    return share * BLOCK + extra * HALF + PAD


def invert_kernel(hidden_blocks, blocks, dp_count, token_total, sweeps, *refs):
    out = refs[-1]
    row, col = masks()
    share, extra = shares(blocks, dp_count)
    slots = share + extra
    me = lax.axis_index("dp")
    factors = summed_factors(refs[:-1], slots, token_total, row, col)
    counts = [
        sweeps[0, hidden_blocks + owned_block(me, j, blocks, dp_count)] for j in range(slots)
    ]
    lines = jnp.zeros((PAD, HALF), jnp.float32)
    place = lax.broadcasted_iota(jnp.int32, (PAD, HALF), 0)
    even = me % 2 == 0
    for j, full in enumerate(newton(factors, counts)):
        upper, mixed, line = pack_block(full, row, col)
        lines = jnp.where(place == j, line, lines)
        if j < share:
            out[pl.ds(j * BLOCK, HALF)] = upper.astype(out.dtype)
            out[pl.ds(j * BLOCK + HALF, HALF)] = mixed.astype(out.dtype)
        else:
            own = jnp.where(even, upper, mixed)
            out[pl.ds(share * BLOCK + (j - share) * HALF, HALF)] = own.astype(out.dtype)
    out[pl.ds(share * BLOCK + extra * HALF, PAD)] = lines.astype(out.dtype)


def in_vmem(arrays):
    return [pltpu.with_memory_space_constraint(array, pltpu.VMEM) for array in arrays]


def invert_units(sweeps, arrays, hidden_blocks, blocks, dp_count, token_total):
    unit = gather_rows(blocks, dp_count)
    slots = sum(shares(blocks, dp_count))
    return pl.pallas_call(
        functools.partial(invert_kernel, hidden_blocks, blocks, dp_count, token_total),
        out_shape=pltpu.VMEM((unit, HALF), jnp.bfloat16),
        grid_spec=pltpu.PrefetchScalarGridSpec(
            num_scalar_prefetch=1,
            grid=(1,),
            in_specs=[pl.BlockSpec(memory_space=pltpu.VMEM)] * len(arrays),
            out_specs=pl.BlockSpec(memory_space=pltpu.VMEM),
        ),
        compiler_params=pltpu.CompilerParams(vmem_limit_bytes=16 << 20),
        cost_estimate=pl.CostEstimate(
            flops=12 * slots * BLOCK**3, bytes_accessed=12 * slots * BLOCK * BLOCK, transcendentals=0
        ),
    )(sweeps, *in_vmem(arrays))


def load_kernel(source, out, sem):
    copy = pltpu.make_async_copy(source.at[0, pl.ds(0, out.shape[0])], out, sem)
    copy.start()
    copy.wait()


def load_rows(source, rows):
    width = source.shape[2]
    return pl.pallas_call(
        load_kernel,
        out_shape=pltpu.VMEM((rows, width), source.dtype),
        in_specs=[pl.BlockSpec(memory_space=pltpu.HBM)],
        out_specs=pl.BlockSpec(memory_space=pltpu.VMEM),
        scratch_shapes=[pltpu.SemaphoreType.DMA],
        compiler_params=pltpu.CompilerParams(vmem_limit_bytes=16 << 20),
        cost_estimate=pl.CostEstimate(flops=0, bytes_accessed=2 * rows * width, transcendentals=0),
    )(pltpu.with_memory_space_constraint(source, pltpu.HBM))


def half_kernel(slots, token_total, sweeps, *refs):
    early, weights, out, late, sem = refs[-5:]
    rows = late.shape[0]
    start = early.shape[0]
    copy = pltpu.make_async_copy(weights.at[0, pl.ds(start, rows)], late, sem)
    copy.start()
    row, col = masks()
    me = lax.axis_index("dp")
    factors = summed_factors(refs[:-5], slots, token_total, row, col)
    found = newton(factors, [sweeps[0, me * slots + j] for j in range(slots)])
    found = [full.astype(jnp.bfloat16) for full in found]
    for part, place in ((early, pl.ds(0, start)), (late, pl.ds(start, rows))):
        if part is late:
            copy.wait()
        for j in range(slots):
            columns = slice(j * BLOCK, (j + 1) * BLOCK)
            value = jnp.dot(part[:, columns], found[j], preferred_element_type=jnp.float32)
            out[place, columns] = value.astype(jnp.bfloat16)


def half_update(sweeps, arrays, token_total, early, weight_grad):
    _, depth, columns = weight_grad.shape
    slots = columns // BLOCK
    specs = [pl.BlockSpec(memory_space=pltpu.VMEM)] * (len(arrays) + 1)
    specs.append(pl.BlockSpec(memory_space=pltpu.HBM))
    return pl.pallas_call(
        functools.partial(half_kernel, slots, token_total),
        out_shape=pltpu.VMEM((depth, columns), jnp.bfloat16),
        grid_spec=pltpu.PrefetchScalarGridSpec(
            num_scalar_prefetch=1,
            grid=(1,),
            in_specs=specs,
            out_specs=pl.BlockSpec(memory_space=pltpu.VMEM),
            scratch_shapes=[
                pltpu.VMEM((depth - early.shape[0], columns), jnp.bfloat16),
                pltpu.SemaphoreType.DMA,
            ],
        ),
        compiler_params=pltpu.CompilerParams(vmem_limit_bytes=24 << 20),
        cost_estimate=pl.CostEstimate(
            flops=12 * slots * BLOCK**3 + 2 * depth * columns * BLOCK,
            bytes_accessed=2 * depth * columns,
            transcendentals=0,
        ),
    )(
        sweeps,
        *in_vmem(arrays),
        pltpu.with_memory_space_constraint(early, pltpu.VMEM),
        pltpu.with_memory_space_constraint(weight_grad, pltpu.HBM),
    )


def update_kernel(blocks, dp_count, cores, turns, places, *refs):
    half, out, staged, sems = refs[-4:]
    units = dict(zip([r + core for core in cores for r in turns], refs))
    share, extra = shares(blocks, dp_count)
    me = lax.axis_index("dp")
    row, col = masks()
    even = me % 2 == 0

    def copy(step, block):
        place = pl.ds(pl.multiple_of(block * BLOCK, BLOCK), BLOCK)
        return pltpu.make_async_copy(staged.at[step], out.at[0, place], sems.at[step])

    def tile(unit, start, rows=HALF):
        return unit[start : start + rows, :].astype(jnp.float32)

    def one(step, r, slot):
        near, far = units.get(r), units.get(r + 1)
        owner = me ^ r
        if slot >= 2 * share:
            slot -= share
            start = share * BLOCK + (slot - share) * HALF
            own, other = tile(near, start), tile(far, start)
            upper, mixed = jnp.where(even, own, other), jnp.where(even, other, own)
        else:
            if slot >= share:
                near, owner, slot = far, owner ^ 1, slot - share
            upper, mixed = tile(near, slot * BLOCK), tile(near, slot * BLOCK + HALF)
        block = owned_block(owner, slot, blocks, dp_count)
        line = tile(near, share * BLOCK + extra * HALF, PAD)[slot : slot + 1]
        full = unpack_block(upper, mixed, line, row, col).astype(jnp.bfloat16)
        place = pl.ds(pl.multiple_of(block * BLOCK, BLOCK), BLOCK)
        value = jnp.dot(full, half[place, :], preferred_element_type=jnp.float32)
        staged[step] = value.astype(jnp.bfloat16)
        copy(step, block).start()

    def guarded(r, slot, run):
        chips, rest = dp_count // 2, blocks % dp_count
        if slot < 2 * share or rest == chips * extra:
            run()
        else:
            pl.when((me ^ r) // 2 + chips * (slot - 2 * share) < rest)(run)

    steps = [(r, slot) for r in turns for slot in places]
    for step, (r, slot) in enumerate(steps):
        guarded(r, slot, functools.partial(one, step, r, slot))
    for step, (r, slot) in enumerate(steps):
        guarded(r, slot, lambda: copy(step, 0).wait())


def update_rows(even, odd, half, dp_count, turns, places, done=None):
    depth, columns = half.shape
    blocks = depth // BLOCK
    steps = len(turns) * len(places)
    units = [*even, *odd]
    operands = units + ([] if done is None else [done])
    specs = [pl.BlockSpec(memory_space=pltpu.VMEM)] * len(units)
    specs += [pl.BlockSpec(memory_space=pl.ANY)] * (len(operands) - len(specs))
    cores = (0, 1) if odd else (0,)
    return pl.pallas_call(
        functools.partial(update_kernel, blocks, dp_count, cores, turns, places),
        out_shape=jax.ShapeDtypeStruct((1, depth, columns), jnp.bfloat16),
        in_specs=specs + [pl.BlockSpec(memory_space=pltpu.VMEM)],
        out_specs=pl.BlockSpec(memory_space=pl.ANY),
        scratch_shapes=[
            pltpu.VMEM((steps, BLOCK, columns), jnp.bfloat16),
            pltpu.SemaphoreType.DMA((steps,)),
        ],
        input_output_aliases={} if done is None else {len(units): 0},
        compiler_params=pltpu.CompilerParams(vmem_limit_bytes=24 << 20),
        cost_estimate=pl.CostEstimate(
            flops=2 * steps * BLOCK * BLOCK * columns,
            bytes_accessed=2 * steps * BLOCK * columns,
            transcendentals=0,
        ),
    )(*operands, pltpu.with_memory_space_constraint(half, pltpu.VMEM))


def swap(value, distance):
    count = lax.axis_size("dp")
    return lax.ppermute(value, "dp", [(i, i ^ distance) for i in range(count)])


def spread(keep, first, dp_count):
    others = []
    for r in range(2, dp_count, 2):
        value = keep[r // 2].astype(jnp.float32) + first[r // 2].astype(jnp.float32)
        others.append(swap(value.astype(jnp.bfloat16), r))
    return others


def whole(acts, input_grads, head_grads, weight_grad, sweeps):
    dp_count = lax.axis_size("dp")
    section_count = lax.axis_size("section")
    tokens = acts.shape[1] * dp_count
    hidden_blocks = acts.shape[2] // BLOCK
    model_blocks = input_grads.shape[2] // BLOCK
    back = [((s + 1) % section_count, s) for s in range(section_count)]
    ahead = [(s, (s + 1) % section_count) for s in range(section_count)]

    send_g, keep_g, early = model_factors(input_grads, head_grads, acts, dp_count)
    first_g = swap(send_g, 1)
    their_sweeps = lax.ppermute(sweeps, "section", ahead)
    send_a, keep_a = hidden_factors(early, acts, dp_count)
    others_g = spread(keep_g, first_g, dp_count)
    first_a = swap(send_a, 1)
    unit = invert_units(
        their_sweeps,
        [keep_g, first_g, *others_g],
        hidden_blocks,
        model_blocks,
        dp_count,
        tokens,
    )
    others_a = spread(keep_a, first_a, dp_count)
    unit = lax.ppermute(unit, "section", back)
    weights = load_rows(weight_grad, weight_grad.shape[1] // 5 * 3)
    even = [unit] + [swap(unit, r) for r in range(2, dp_count, 2)]
    half = half_update(sweeps, [keep_a, first_a, *others_a], tokens, weights, weight_grad)
    odd = [swap(unit, 1)]
    odd += [swap(value, 1) for value in even[1:]]
    share, extra = shares(model_blocks, dp_count)
    turns, places = list(range(0, dp_count, 2)), list(range(2 * share + extra))
    return update_rows(even, odd, half, dp_count, turns, places)


def solution(mesh):
    return jax.shard_map(
        whole,
        mesh=mesh,
        in_specs=(
            P("section", "dp", None),
            P("section", "dp", None),
            P("dp", None),
            P("section", None, "dp"),
            P("section", None),
        ),
        out_specs=P("section", None, "dp"),
        check_vma=False,
    )
```

```python
import functools

import jax
import jax.numpy as jnp
from jax import lax
from jax.experimental import pallas as pl
from jax.experimental.pallas import tpu as pltpu
from jax.sharding import PartitionSpec as P


BLOCK = 256
HALF = BLOCK // 2
PAD = 16
NS_MAX = 4

damping = 0.05

KEEP_PART = 4.0


def masks():
    row = lax.broadcasted_iota(jnp.int32, (HALF, HALF), 0)
    col = lax.broadcasted_iota(jnp.int32, (HALF, HALF), 1)
    return row, col


def pack_block(full, row, col):
    upper = full[:HALF, HALF:]
    second = full[HALF:, HALF:]
    mixed = jnp.where(row >= col, full[:HALF, :HALF], second)
    line = jnp.sum(jnp.where(row == col, second, 0.0), axis=0, keepdims=True)
    return upper, mixed, line


def unpack_block(upper, mixed, line, row, col):
    turned = mixed.T
    first = jnp.where(row >= col, mixed, turned)
    second = jnp.where(row < col, mixed, jnp.where(row > col, turned, line))
    top = jnp.concatenate([first, upper], axis=1)
    bottom = jnp.concatenate([upper.T, second], axis=1)
    return jnp.concatenate([top, bottom], axis=0)


def store_unit(out, index, blocks, row, col):
    count = len(blocks)
    lines = jnp.zeros((PAD, HALF), jnp.float32)
    place = lax.broadcasted_iota(jnp.int32, (PAD, HALF), 0)
    for j, full in enumerate(blocks):
        upper, mixed, line = pack_block(full, row, col)
        out[index + (pl.ds(j * BLOCK, HALF),)] = upper.astype(out.dtype)
        out[index + (pl.ds(j * BLOCK + HALF, HALF),)] = mixed.astype(out.dtype)
        lines = jnp.where(place == j, line, lines)
    out[index + (pl.ds(count * BLOCK, PAD),)] = lines.astype(out.dtype)


def gram(x):
    return lax.dot_general(x, x, (((0,), (0,)), ((), ())), preferred_element_type=jnp.float32)


def shares(blocks, dp_count):
    share, rest = blocks // dp_count, blocks % dp_count
    return share, -(-rest // (dp_count // 2))


def owned_block(owner, slot, blocks, dp_count):
    share, _ = shares(blocks, dp_count)
    if slot < share:
        return owner * share + slot
    chips = dp_count // 2
    return jnp.minimum(share * dp_count + owner // 2 + chips * (slot - share), blocks - 1)


def store_factors(columns, out, parity, blocks, dp_count, row, col, chips=None):
    me = lax.axis_index("dp")
    for place, step in enumerate(range(dp_count // 2) if chips is None else chips):
        grams = []
        for slot in range(sum(shares(blocks, dp_count))):
            block = owned_block(me ^ (2 * step + parity), slot, blocks, dp_count)
            span = pl.ds(pl.multiple_of(block * BLOCK, BLOCK), BLOCK)
            grams.append(sum(gram(part[:, span]) for part in columns))
        store_unit(out, (place,), grams, row, col)


def send_kernel(blocks, dp_count, here, head, sent_far, sent_near, grads, sems):
    chunks = sems.shape[0]
    rows = grads.shape[0] // chunks

    def fetch(source, i):
        place = pl.ds(i * rows, rows)
        view = source.at[0, place] if len(source.shape) == 3 else source.at[place]
        return pltpu.make_async_copy(view, grads.at[place], sems.at[i])

    def fetch_all(source):
        for i in range(chunks):
            fetch(source, i).start()

    first = lax.axis_index("section") == 0
    pl.when(first)(lambda: fetch_all(head))
    pl.when(jnp.logical_not(first))(lambda: fetch_all(here))
    for i in range(chunks):
        fetch(here, i).wait()
    far, near = far_and_near(dp_count)
    store_factors([grads], sent_far, 1, blocks, dp_count, *masks(), far)
    store_factors([grads], sent_near, 1, blocks, dp_count, *masks(), near)


def far_and_near(dp_count):
    chips = range(dp_count // 2)
    return [c for c in chips if c.bit_count() > 1], [c for c in chips if c.bit_count() < 2]


def half_of_kernel(blocks, dp_count, parity, columns, out):
    view = columns.at[0] if len(columns.shape) == 3 else columns
    store_factors([view], out, parity, blocks, dp_count, *masks())


def packed_shape(blocks, dp_count, chips=None):
    unit = sum(shares(blocks, dp_count)) * BLOCK + PAD
    return pltpu.VMEM((chips or dp_count // 2, unit, HALF), jnp.bfloat16)


def factor_call(kernel, operands, spaces, outs, scratch, rows, width, part):
    return pl.pallas_call(
        kernel,
        out_shape=outs,
        in_specs=[pl.BlockSpec(memory_space=space) for space in spaces],
        out_specs=tuple(pl.BlockSpec(memory_space=pltpu.VMEM) for _ in outs),
        scratch_shapes=scratch,
        compiler_params=pltpu.CompilerParams(vmem_limit_bytes=16 << 20),
        cost_estimate=pl.CostEstimate(
            flops=int(2 * part * rows * width * BLOCK), bytes_accessed=rows * width * 3, transcendentals=0
        ),
    )(
        *[
            pltpu.with_memory_space_constraint(operand, space)
            for operand, space in zip(operands, spaces)
        ]
    )


def half_of_factors(columns, parity, dp_count, part=0.5):
    rows, width = columns.shape[-2:]
    (packed,) = factor_call(
        functools.partial(half_of_kernel, width // BLOCK, dp_count, parity),
        [columns],
        [pltpu.VMEM],
        (packed_shape(width // BLOCK, dp_count),),
        [],
        rows,
        width,
        part,
    )
    return packed


def model_factors(input_grads, head_grads, dp_count):
    rows, width = head_grads.shape
    shapes = [packed_shape(width // BLOCK, dp_count, len(c)) for c in far_and_near(dp_count)]
    far, near, grads = factor_call(
        functools.partial(send_kernel, width // BLOCK, dp_count),
        [input_grads, head_grads],
        [pltpu.HBM] * 2,
        (*shapes, pltpu.VMEM((rows, width), jnp.bfloat16)),
        [pltpu.SemaphoreType.DMA((4,))],
        rows,
        width,
        0.5,
    )
    kept = half_of_factors(grads, 0, dp_count, KEEP_PART)
    return far, near, kept


def hidden_factors(acts, dp_count):
    sent = half_of_factors(acts, 1, dp_count)
    kept = half_of_factors(acts, 0, dp_count)
    return sent, kept


def product(a, b):
    return jnp.dot(
        a.astype(jnp.bfloat16), b.astype(jnp.bfloat16), preferred_element_type=jnp.float32
    )


def newton(matrices, counts):
    row = lax.broadcasted_iota(jnp.int32, (BLOCK, BLOCK), 0)
    col = lax.broadcasted_iota(jnp.int32, (BLOCK, BLOCK), 1)
    diagonal = row == col
    levels, rest, heights, found = [], [], [], []
    for matrix in matrices:
        size = jnp.sum(jnp.abs(matrix), axis=0, keepdims=True)
        scale = 1.0 / jnp.max(size, axis=1, keepdims=True)
        line = jnp.sum(jnp.where(diagonal, matrix, 0.0), axis=0, keepdims=True)
        shift = scale * jnp.sum(line, axis=1, keepdims=True) * (1.0 / BLOCK)
        left = jnp.where(diagonal, shift, 0.0) - scale * matrix
        levels.append(1.0 - shift)
        rest.append(left)
        heights.append(scale * (2.0 - shift))
        found.append(scale * left)
    for turn in range(1, NS_MAX):
        rest = [2.0 * a * left + product(left, left) for a, left in zip(levels, rest)]
        levels = [a * a for a in levels]
        step = [
            x * left + a * part + product(part, left)
            for a, left, x, part in zip(levels, rest, heights, found)
        ]
        more = [turn < count for count in counts]
        found = [jnp.where(go, part + add, part) for go, part, add in zip(more, found, step)]
        heights = [jnp.where(go, x + a * x, x) for go, x, a in zip(more, heights, levels)]
    return [part + jnp.where(diagonal, x, 0.0) for x, part in zip(heights, found)]


def summed_factors(refs, slots, token_total, row, col):
    terms = [ref[0] if len(ref.shape) == 3 else ref[...] for ref in refs]
    total = sum(term.astype(jnp.float32) for term in terms) * (1.0 / token_total)
    wide_row = lax.broadcasted_iota(jnp.int32, (BLOCK, BLOCK), 0)
    wide_col = lax.broadcasted_iota(jnp.int32, (BLOCK, BLOCK), 1)
    shift = jnp.where(wide_row == wide_col, damping, 0.0)
    blocks = []
    for j in range(slots):
        upper = total[j * BLOCK : j * BLOCK + HALF]
        mixed = total[j * BLOCK + HALF : (j + 1) * BLOCK]
        line = total[slots * BLOCK + j : slots * BLOCK + j + 1]
        blocks.append(unpack_block(upper, mixed, line, row, col) + shift)
    return blocks


def gather_rows(blocks, dp_count):
    share, extra = shares(blocks, dp_count)
    return share * BLOCK + extra * HALF + PAD


def invert_kernel(hidden_blocks, blocks, dp_count, token_total, sweeps, *refs):
    out = refs[-1]
    row, col = masks()
    share, extra = shares(blocks, dp_count)
    slots = share + extra
    me = lax.axis_index("dp")
    factors = summed_factors(refs[:-1], slots, token_total, row, col)
    counts = [
        sweeps[0, hidden_blocks + owned_block(me, j, blocks, dp_count)] for j in range(slots)
    ]
    lines = jnp.zeros((PAD, HALF), jnp.float32)
    place = lax.broadcasted_iota(jnp.int32, (PAD, HALF), 0)
    even = me % 2 == 0
    for j, full in enumerate(newton(factors, counts)):
        upper, mixed, line = pack_block(full, row, col)
        lines = jnp.where(place == j, line, lines)
        if j < share:
            out[pl.ds(j * BLOCK, HALF)] = upper.astype(out.dtype)
            out[pl.ds(j * BLOCK + HALF, HALF)] = mixed.astype(out.dtype)
        else:
            own = jnp.where(even, upper, mixed)
            out[pl.ds(share * BLOCK + (j - share) * HALF, HALF)] = own.astype(out.dtype)
    out[pl.ds(share * BLOCK + extra * HALF, PAD)] = lines.astype(out.dtype)


def in_vmem(arrays):
    return [pltpu.with_memory_space_constraint(array, pltpu.VMEM) for array in arrays]


def invert_units(sweeps, arrays, hidden_blocks, blocks, dp_count, token_total):
    unit = gather_rows(blocks, dp_count)
    slots = sum(shares(blocks, dp_count))
    return pl.pallas_call(
        functools.partial(invert_kernel, hidden_blocks, blocks, dp_count, token_total),
        out_shape=pltpu.VMEM((unit, HALF), jnp.bfloat16),
        grid_spec=pltpu.PrefetchScalarGridSpec(
            num_scalar_prefetch=1,
            grid=(1,),
            in_specs=[pl.BlockSpec(memory_space=pltpu.VMEM)] * len(arrays),
            out_specs=pl.BlockSpec(memory_space=pltpu.VMEM),
        ),
        compiler_params=pltpu.CompilerParams(vmem_limit_bytes=16 << 20),
        cost_estimate=pl.CostEstimate(
            flops=12 * slots * BLOCK**3, bytes_accessed=12 * slots * BLOCK * BLOCK, transcendentals=0
        ),
    )(sweeps, *in_vmem(arrays))


def load_kernel(source, out, sem):
    copy = pltpu.make_async_copy(source.at[0, pl.ds(0, out.shape[0])], out, sem)
    copy.start()
    copy.wait()


def load_rows(source, rows):
    width = source.shape[2]
    return pl.pallas_call(
        load_kernel,
        out_shape=pltpu.VMEM((rows, width), source.dtype),
        in_specs=[pl.BlockSpec(memory_space=pltpu.HBM)],
        out_specs=pl.BlockSpec(memory_space=pltpu.VMEM),
        scratch_shapes=[pltpu.SemaphoreType.DMA],
        compiler_params=pltpu.CompilerParams(vmem_limit_bytes=16 << 20),
        cost_estimate=pl.CostEstimate(flops=0, bytes_accessed=2 * rows * width, transcendentals=0),
    )(pltpu.with_memory_space_constraint(source, pltpu.HBM))


def half_kernel(slots, token_total, sweeps, *refs):
    early, weights, out, late, sem = refs[-5:]
    rows = late.shape[0]
    start = early.shape[0]
    copy = pltpu.make_async_copy(weights.at[0, pl.ds(start, rows)], late, sem)
    copy.start()
    row, col = masks()
    me = lax.axis_index("dp")
    factors = summed_factors(refs[:-5], slots, token_total, row, col)
    found = newton(factors, [sweeps[0, me * slots + j] for j in range(slots)])
    found = [full.astype(jnp.bfloat16) for full in found]
    for part, place in ((early, pl.ds(0, start)), (late, pl.ds(start, rows))):
        if part is late:
            copy.wait()
        for j in range(slots):
            columns = slice(j * BLOCK, (j + 1) * BLOCK)
            value = jnp.dot(part[:, columns], found[j], preferred_element_type=jnp.float32)
            out[place, columns] = value.astype(jnp.bfloat16)


def half_update(sweeps, arrays, token_total, early, weight_grad):
    _, depth, columns = weight_grad.shape
    slots = columns // BLOCK
    specs = [pl.BlockSpec(memory_space=pltpu.VMEM)] * (len(arrays) + 1)
    specs.append(pl.BlockSpec(memory_space=pltpu.HBM))
    return pl.pallas_call(
        functools.partial(half_kernel, slots, token_total),
        out_shape=pltpu.VMEM((depth, columns), jnp.bfloat16),
        grid_spec=pltpu.PrefetchScalarGridSpec(
            num_scalar_prefetch=1,
            grid=(1,),
            in_specs=specs,
            out_specs=pl.BlockSpec(memory_space=pltpu.VMEM),
            scratch_shapes=[
                pltpu.VMEM((depth - early.shape[0], columns), jnp.bfloat16),
                pltpu.SemaphoreType.DMA,
            ],
        ),
        compiler_params=pltpu.CompilerParams(vmem_limit_bytes=24 << 20),
        cost_estimate=pl.CostEstimate(
            flops=12 * slots * BLOCK**3 + 2 * depth * columns * BLOCK,
            bytes_accessed=2 * depth * columns,
            transcendentals=0,
        ),
    )(
        sweeps,
        *in_vmem(arrays),
        pltpu.with_memory_space_constraint(early, pltpu.VMEM),
        pltpu.with_memory_space_constraint(weight_grad, pltpu.HBM),
    )


def update_kernel(blocks, dp_count, cores, turns, places, *refs):
    half, out, staged, sems = refs[-4:]
    units = dict(zip([r + core for core in cores for r in turns], refs))
    share, extra = shares(blocks, dp_count)
    me = lax.axis_index("dp")
    row, col = masks()
    even = me % 2 == 0

    def copy(step, block):
        place = pl.ds(pl.multiple_of(block * BLOCK, BLOCK), BLOCK)
        return pltpu.make_async_copy(staged.at[step], out.at[0, place], sems.at[step])

    def tile(unit, start, rows=HALF):
        return unit[start : start + rows, :].astype(jnp.float32)

    def one(step, r, slot):
        near, far = units.get(r), units.get(r + 1)
        owner = me ^ r
        if slot >= 2 * share:
            slot -= share
            start = share * BLOCK + (slot - share) * HALF
            own, other = tile(near, start), tile(far, start)
            upper, mixed = jnp.where(even, own, other), jnp.where(even, other, own)
        else:
            if slot >= share:
                near, owner, slot = far, owner ^ 1, slot - share
            upper, mixed = tile(near, slot * BLOCK), tile(near, slot * BLOCK + HALF)
        block = owned_block(owner, slot, blocks, dp_count)
        line = tile(near, share * BLOCK + extra * HALF, PAD)[slot : slot + 1]
        full = unpack_block(upper, mixed, line, row, col).astype(jnp.bfloat16)
        place = pl.ds(pl.multiple_of(block * BLOCK, BLOCK), BLOCK)
        value = jnp.dot(full, half[place, :], preferred_element_type=jnp.float32)
        staged[step] = value.astype(jnp.bfloat16)
        copy(step, block).start()

    def guarded(r, slot, run):
        chips, rest = dp_count // 2, blocks % dp_count
        if slot < 2 * share or rest == chips * extra:
            run()
        else:
            pl.when((me ^ r) // 2 + chips * (slot - 2 * share) < rest)(run)

    steps = [(r, slot) for r in turns for slot in places]
    for step, (r, slot) in enumerate(steps):
        guarded(r, slot, functools.partial(one, step, r, slot))
    for step, (r, slot) in enumerate(steps):
        guarded(r, slot, lambda: copy(step, 0).wait())


def update_rows(even, odd, half, dp_count, turns, places, done=None):
    depth, columns = half.shape
    blocks = depth // BLOCK
    steps = len(turns) * len(places)
    units = [*even, *odd]
    operands = units + ([] if done is None else [done])
    specs = [pl.BlockSpec(memory_space=pltpu.VMEM)] * len(units)
    specs += [pl.BlockSpec(memory_space=pl.ANY)] * (len(operands) - len(specs))
    cores = (0, 1) if odd else (0,)
    return pl.pallas_call(
        functools.partial(update_kernel, blocks, dp_count, cores, turns, places),
        out_shape=jax.ShapeDtypeStruct((1, depth, columns), jnp.bfloat16),
        in_specs=specs + [pl.BlockSpec(memory_space=pltpu.VMEM)],
        out_specs=pl.BlockSpec(memory_space=pl.ANY),
        scratch_shapes=[
            pltpu.VMEM((steps, BLOCK, columns), jnp.bfloat16),
            pltpu.SemaphoreType.DMA((steps,)),
        ],
        input_output_aliases={} if done is None else {len(units): 0},
        compiler_params=pltpu.CompilerParams(vmem_limit_bytes=24 << 20),
        cost_estimate=pl.CostEstimate(
            flops=2 * steps * BLOCK * BLOCK * columns,
            bytes_accessed=2 * steps * BLOCK * columns,
            transcendentals=0,
        ),
    )(*operands, pltpu.with_memory_space_constraint(half, pltpu.VMEM))


def swap(value, distance):
    count = lax.axis_size("dp")
    return lax.ppermute(value, "dp", [(i, i ^ distance) for i in range(count)])


def chip_sums(keep, first, chips):
    sums = {}
    for place, chip in enumerate(chips):
        if chip:
            value = keep[chip].astype(jnp.float32) + first[place].astype(jnp.float32)
            sums[chip] = value.astype(jnp.bfloat16)
    return sums


def spread(sums):
    return [swap(value, 2 * chip) for chip, value in sums.items()]


def whole(acts, input_grads, head_grads, weight_grad, sweeps):
    dp_count = lax.axis_size("dp")
    section_count = lax.axis_size("section")
    tokens = acts.shape[1] * dp_count
    hidden_blocks = acts.shape[2] // BLOCK
    model_blocks = input_grads.shape[2] // BLOCK
    back = [((s + 1) % section_count, s) for s in range(section_count)]
    ahead = [(s, (s + 1) % section_count) for s in range(section_count)]

    far_g, near_g, keep_g = model_factors(input_grads, head_grads, dp_count)
    far, near = far_and_near(dp_count)
    far_g = swap(far_g, 1)
    first_g = swap(near_g, 1)
    their_sweeps = lax.ppermute(sweeps, "section", ahead)
    send_a, keep_a = hidden_factors(acts, dp_count)
    sums = chip_sums(keep_g, far_g, far)
    sums, later = lax.optimization_barrier((sums, keep_g))
    others_g = spread(sums)
    others_g += spread(chip_sums(later, first_g, near))
    first_a = swap(send_a, 1)
    unit = invert_units(
        their_sweeps,
        [keep_g, first_g, *others_g],
        hidden_blocks,
        model_blocks,
        dp_count,
        tokens,
    )
    others_a = spread(chip_sums(keep_a, first_a, range(dp_count // 2)))
    unit = lax.ppermute(unit, "section", back)
    weights = load_rows(weight_grad, weight_grad.shape[1] // 5 * 3)
    even = [unit] + [swap(unit, r) for r in range(dp_count - 2, 0, -2)][::-1]
    half = half_update(sweeps, [keep_a, first_a, *others_a], tokens, weights, weight_grad)
    odd = [swap(unit, 1)]
    odd += [swap(value, 1) for value in even[1:]]
    share, extra = shares(model_blocks, dp_count)
    turns, places = list(range(0, dp_count, 2)), list(range(2 * share + extra))
    return update_rows(even, odd, half, dp_count, turns, places)


def solution(mesh):
    return jax.shard_map(
        whole,
        mesh=mesh,
        in_specs=(
            P("section", "dp", None),
            P("section", "dp", None),
            P("dp", None),
            P("section", None, "dp"),
            P("section", None),
        ),
        out_specs=P("section", None, "dp"),
        check_vma=False,
    )
```
